32 devices in a mesh: batch: 8 (over z, x), head: 4 (over y, core).
Axes of the slice: x: 2, y: 2, z: 4, core: 2. Of those that a mesh axis runs over, the one named last changes fastest.
Arguments:
- tokens: bfloat16 [2, 8, 1024, 768], P(None, 'batch', 'head'), may hold values from -6 to 6
- memory: bfloat16 [2, 8, 1024, 768], P(None, 'batch', 'head'), may hold values from -6 to 6
- cotangent: bfloat16 [2, 8, 1024, 768], P(None, 'batch', 'head'), may hold values from -6 to 6
- bucket: int32 [2, 8], P(None, 'batch'), may hold values from 0 to 1, as said below
- target_count: int32 [2, 8, 4], P(None, 'batch'), may hold values from 153 to 256, as said below
- memory_count: int32 [2, 8, 4], P(None, 'batch'), may hold values from 153 to 256, as said below
- self_weight: bfloat16 [768, 2304], P(('batch', 'head')), may hold values from -0.21875 to 0.21875
- query_bias: bfloat16 [768], P(('batch', 'head')), may hold values from -3 to 3
- value_bias: bfloat16 [768], P(('batch', 'head')), may hold values from -3 to 3
- attend_weight: bfloat16 [768, 768], P(('batch', 'head')), may hold values from -0.875 to 0.875
- attend_bias: bfloat16 [768], P(('batch', 'head')), may hold values from -3 to 3
- first_gain: bfloat16 [768], P(('batch', 'head')), may hold values from 0.5 to 1.5
- first_shift: bfloat16 [768], P(('batch', 'head')), may hold values from -2 to 2
- cross_query: bfloat16 [768, 768], P(('batch', 'head')), may hold values from -0.21875 to 0.21875
- cross_bias: bfloat16 [768], P(('batch', 'head')), may hold values from -3 to 3
- memory_weight: bfloat16 [768, 1536], P(('batch', 'head')), may hold values from -0.21875 to 0.21875
- memory_bias: bfloat16 [768], P(('batch', 'head')), may hold values from -3 to 3
- cross_weight: bfloat16 [768, 768], P(('batch', 'head')), may hold values from -0.875 to 0.875
- crossed_bias: bfloat16 [768], P(('batch', 'head')), may hold values from -3 to 3
- second_gain: bfloat16 [768], P(('batch', 'head')), may hold values from 0.5 to 1.5
- second_shift: bfloat16 [768], P(('batch', 'head')), may hold values from -2 to 2
- expand_weight: bfloat16 [768, 3072], P(('batch', 'head')), may hold values from -0.21875 to 0.21875
- expand_bias: bfloat16 [3072], P(('batch', 'head')), may hold values from -3 to 3
- reduce_weight: bfloat16 [3072, 768], P(('batch', 'head')), may hold values from -0.109375 to 0.109375
- reduce_bias: bfloat16 [768], P(('batch', 'head')), may hold values from -3 to 3
- third_gain: bfloat16 [768], P(('batch', 'head')), may hold values from 0.5 to 1.5
- third_shift: bfloat16 [768], P(('batch', 'head')), may hold values from -2 to 2
Outputs:
- output: bfloat16 [2, 8, 1024, 768], P(None, 'batch', 'head')
- tokens_grad: float32 [2, 8, 1024, 768], P(None, 'batch', 'head')
- memory_grad: float32 [2, 8, 1024, 768], P(None, 'batch', 'head')
- self_weight_grad: float32 [768, 2304], P(('batch', 'head'))
- query_bias_grad: float32 [768], P(('batch', 'head'))
- value_bias_grad: float32 [768], P(('batch', 'head'))
- attend_weight_grad: float32 [768, 768], P(('batch', 'head'))
- attend_bias_grad: float32 [768], P(('batch', 'head'))
- first_gain_grad: float32 [768], P(('batch', 'head'))
- first_shift_grad: float32 [768], P(('batch', 'head'))
- cross_query_grad: float32 [768, 768], P(('batch', 'head'))
- cross_bias_grad: float32 [768], P(('batch', 'head'))
- memory_weight_grad: float32 [768, 1536], P(('batch', 'head'))
- memory_bias_grad: float32 [768], P(('batch', 'head'))
- cross_weight_grad: float32 [768, 768], P(('batch', 'head'))
- crossed_bias_grad: float32 [768], P(('batch', 'head'))
- second_gain_grad: float32 [768], P(('batch', 'head'))
- second_shift_grad: float32 [768], P(('batch', 'head'))
- expand_weight_grad: float32 [768, 3072], P(('batch', 'head'))
- expand_bias_grad: float32 [3072], P(('batch', 'head'))
- reduce_weight_grad: float32 [3072, 768], P(('batch', 'head'))
- reduce_bias_grad: float32 [768], P(('batch', 'head'))
- third_gain_grad: float32 [768], P(('batch', 'head'))
- third_shift_grad: float32 [768], P(('batch', 'head'))
The draws below stay inside these ranges and needn't reach their ends.
Inputs may be any that keep to these rules, and one draw needn't show every extreme that they name: `bucket`: 1 marks a micro-batch of a batch index whose rows are 4 rows of 256 slots each, 0 one whose rows are single rows of 1024 slots. `target_count`: live slots come first in each quarter; under bucket 0 all quarters but the last are full, so a row's live slots are one prefix. `memory_count`: live slots come first in each quarter; under bucket 0 all quarters but the last are full, so a row's live slots are one prefix.
All inputs are finite; a program needn't handle non-finite values.
Results may differ from the reference program's by a relative error of at most 0.024.
Values may be sent and summed in bfloat16 or wider, within the bound.
No kernel may reach another device: no remote copies, remote signals or barrier semaphores. Data moves between devices by JAX's collectives and lax.ppermute only.
A program may use at most 256 MiB of HBM per device.

```python
import jax
import jax.numpy as jnp
from jax import lax

D = 768
HEADS = 12
HD = 64
FF = 3072
SHORT = 256
ROWS = 1
MICRO = 2
GROUPS = 8
NROWS = 8
QUARTERS = 4
LONG = 1024


def bucket_common(key):
    return jax.random.randint(jax.random.fold_in(key, 7), (MICRO, GROUPS), 0, 2, dtype=jnp.int32)


def count_common(key, offset_seed):
    row_kinds = jnp.repeat(bucket_common(key), ROWS, axis=1)
    short_counts = jax.random.randint(jax.random.fold_in(key, offset_seed), (MICRO, NROWS, QUARTERS), SHORT - SHORT // 5, SHORT + 1, dtype=jnp.int32)
    tail_counts = jax.random.randint(jax.random.fold_in(key, offset_seed + 1), (MICRO, NROWS, QUARTERS), SHORT * 3 // 5, SHORT + 1, dtype=jnp.int32)
    last_quarter = jnp.arange(QUARTERS, dtype=jnp.int32) == QUARTERS - 1
    long_counts = jnp.where(last_quarter[None, None, :], tail_counts, SHORT)
    return jnp.where(row_kinds[:, :, None] == 1, short_counts, long_counts).astype(jnp.int32)


def draw_bucket(key, part):
    return bucket_common(key)


def draw_target_count(key, part):
    return count_common(key, 21)


def draw_memory_count(key, part):
    return count_common(key, 41)


def shard_levels(stream_key, dims, shards, smallest, top_value):
    def one(axis_at, blocks):
        draws = jax.random.uniform(jax.random.fold_in(jax.random.fold_in(stream_key, 6), axis_at), (blocks,), jnp.float32, smallest / len(shards), top_value / len(shards))
        return jnp.repeat(jnp.exp(draws), dims[axis_at] // blocks).reshape((-1,) + (1,) * (len(dims) - axis_at - 1))

    level = one(*shards[0])
    for cut in shards[1:]:
        level = level * one(*cut)
    return level


def scatter_about(stream_key, shape, scale, limit, pieces=(), kind=jnp.bfloat16):
    entries = jax.random.normal(stream_key, shape, jnp.float32) * scale
    if len(pieces) > 0:
        entries = shard_levels(stream_key, shape, pieces, -0.22, 0.18) * entries
    return jnp.clip(entries, min=-limit, max=limit).astype(kind)


def setup_inputs(seed: int = 0) -> dict:
    key_of = jax.random.split(jax.random.key(seed), 28)
    return {
        "tokens": scatter_about(key_of[0], (MICRO, NROWS, LONG, D), 1.0, 6.0, ((1, 8), (2, 4))),
        "memory": scatter_about(key_of[1], (MICRO, NROWS, LONG, D), 1.0, 6.0, ((1, 8), (2, 4))),
        "cotangent": scatter_about(key_of[2], (MICRO, NROWS, LONG, D), 1.0, 6.0, ((1, 8), (2, 4))),
        "bucket": draw_bucket(jax.random.fold_in(key_of[27], 71), 0),
        "target_count": draw_target_count(jax.random.fold_in(key_of[27], 71), 0),
        "memory_count": draw_memory_count(jax.random.fold_in(key_of[27], 71), 0),
        "self_weight": scatter_about(key_of[6], (D, 3 * D), D ** -0.5, 0.21875, ((0, 32),)),
        "query_bias": scatter_about(key_of[7], (D,), 0.5, 3.0, ((0, 32),)),
        "value_bias": scatter_about(key_of[8], (D,), 0.5, 3.0, ((0, 32),)),
        "attend_weight": scatter_about(key_of[9], (D, D), (D // 16) ** -0.5, 0.875, ((0, 32),)),
        "attend_bias": scatter_about(key_of[10], (D,), 0.5, 3.0, ((0, 32),)),
        "first_gain": jnp.clip(1.0 + 0.1 * jax.random.normal(key_of[11], (D,), jnp.float32), 0.5, 1.5).astype(jnp.bfloat16),
        "first_shift": scatter_about(key_of[12], (D,), 0.3, 2.0, ((0, 32),)),
        "cross_query": scatter_about(key_of[13], (D, D), D ** -0.5, 0.21875, ((0, 32),)),
        "cross_bias": scatter_about(key_of[14], (D,), 0.5, 3.0, ((0, 32),)),
        "memory_weight": scatter_about(key_of[15], (D, 2 * D), D ** -0.5, 0.21875, ((0, 32),)),
        "memory_bias": scatter_about(key_of[16], (D,), 0.5, 3.0, ((0, 32),)),
        "cross_weight": scatter_about(key_of[17], (D, D), (D // 16) ** -0.5, 0.875, ((0, 32),)),
        "crossed_bias": scatter_about(key_of[18], (D,), 0.5, 3.0, ((0, 32),)),
        "second_gain": jnp.clip(1.0 + 0.1 * jax.random.normal(key_of[19], (D,), jnp.float32), 0.5, 1.5).astype(jnp.bfloat16),
        "second_shift": scatter_about(key_of[20], (D,), 0.3, 2.0, ((0, 32),)),
        "expand_weight": scatter_about(key_of[21], (D, FF), D ** -0.5, 0.21875, ((0, 32),)),
        "expand_bias": scatter_about(key_of[22], (FF,), 0.5, 3.0, ((0, 32),)),
        "reduce_weight": scatter_about(key_of[23], (FF, D), FF ** -0.5, 0.109375, ((0, 32),)),
        "reduce_bias": scatter_about(key_of[24], (D,), 0.5, 3.0, ((0, 32),)),
        "third_gain": jnp.clip(1.0 + 0.1 * jax.random.normal(key_of[25], (D,), jnp.float32), 0.5, 1.5).astype(jnp.bfloat16),
        "third_shift": scatter_about(key_of[26], (D,), 0.3, 2.0, ((0, 32),)),
    }


@jax.custom_vjp
def low(v):
    return lax.optimization_barrier(v.astype(jnp.bfloat16)).astype(jnp.float32)

@jax.custom_vjp
def low_back(v):
    return v

def low_keep(v):
    return (low(v), None)

def low_pass(kept, grad):
    return (grad,)

def back_keep(v):
    return (v, None)

def back_low(kept, grad):
    return (low(grad),)
low.defvjp(low_keep, low_pass)
low_back.defvjp(back_keep, back_low)
exact_mode = lax.Precision.HIGHEST

def matmul(left, right):
    return jnp.dot(left, right, precision=exact_mode)

def rounded(value):
    return low_back(low(value))

def layer_norm(value, gain, shift):
    centre = value - lax.optimization_barrier(jnp.mean(value, axis=-1, keepdims=True))
    spread = lax.optimization_barrier(jnp.mean(centre * centre, axis=-1, keepdims=True))
    return centre * lax.rsqrt(spread + 1e-05) * gain + shift

def row_masks(bucket_value, target_counts, memory_counts):
    slots = jnp.arange(LONG, dtype=jnp.int32)
    segment = jnp.where(bucket_value == 1, slots // SHORT, 0)
    offsets = jnp.arange(SHORT, dtype=jnp.int32)
    target_live = (offsets[None, :] < target_counts[:, None]).reshape(LONG)
    memory_live = (offsets[None, :] < memory_counts[:, None]).reshape(LONG)
    same_part = segment[:, None] == segment[None, :]
    self_mask = same_part & (slots[None, :] <= slots[:, None]) & target_live[None, :]
    cross_mask = same_part & memory_live[None, :]
    return (self_mask, cross_mask)

def attention_row(queries, keys, values, allowed):
    length = queries.shape[0]
    query_heads = queries.reshape(length, HEADS, HD)
    key_heads = keys.reshape(keys.shape[0], HEADS, HD)
    value_heads = values.reshape(values.shape[0], HEADS, HD)
    scores = jnp.einsum('qhd,khd->hqk', query_heads, key_heads, precision=exact_mode) * 0.125
    scores = low_back(scores)
    scores = jnp.where(allowed[None], scores, -1e+30)
    probs = jax.nn.softmax(scores, axis=-1)
    mixed = jnp.einsum('hqk,khd->qhd', low(probs), value_heads, precision=exact_mode)
    return mixed.reshape(length, HEADS * HD)

def layer_row(params, hidden, memory_rows, self_mask, cross_mask):
    self_weight, query_bias, value_bias, attend_weight, attend_bias, first_gain, first_shift, cross_query, cross_bias, memory_weight, memory_bias, cross_weight, crossed_bias, second_gain, second_shift, expand_weight, expand_bias, reduce_weight, reduce_bias, third_gain, third_shift = params
    zero_vector = jnp.zeros_like(query_bias)
    projected = rounded(matmul(hidden, self_weight) + jnp.concatenate([query_bias, zero_vector, value_bias]))
    mixed = rounded(attention_row(projected[:, :D], projected[:, D:2 * D], projected[:, 2 * D:], self_mask))
    attended = low_back(matmul(mixed, attend_weight) + attend_bias)
    first = layer_norm(hidden + attended, first_gain, first_shift)
    cross_queries = rounded(matmul(low(first), cross_query) + cross_bias)
    memory_proj = rounded(matmul(memory_rows, memory_weight) + jnp.concatenate([zero_vector, memory_bias]))
    crossed = rounded(attention_row(cross_queries, memory_proj[:, :D], memory_proj[:, D:], cross_mask))
    crossing = low_back(matmul(crossed, cross_weight) + crossed_bias)
    second = layer_norm(first + crossing, second_gain, second_shift)
    inner = low_back(matmul(low(second), expand_weight) + expand_bias)
    active = low(jax.nn.gelu(inner, approximate=False))
    feeding = low_back(matmul(active, reduce_weight) + reduce_bias)
    return layer_norm(second + feeding, third_gain, third_shift)

def reference(tokens, memory, cotangent, bucket, target_count, memory_count, self_weight, query_bias, value_bias, attend_weight, attend_bias, first_gain, first_shift, cross_query, cross_bias, memory_weight, memory_bias, cross_weight, crossed_bias, second_gain, second_shift, expand_weight, expand_bias, reduce_weight, reduce_bias, third_gain, third_shift):
    params = tuple((entry.astype(jnp.float32) for entry in (self_weight, query_bias, value_bias, attend_weight, attend_bias, first_gain, first_shift, cross_query, cross_bias, memory_weight, memory_bias, cross_weight, crossed_bias, second_gain, second_shift, expand_weight, expand_bias, reduce_weight, reduce_bias, third_gain, third_shift)))
    total_rows = MICRO * NROWS
    flat_tokens = tokens.reshape(total_rows, LONG, D).astype(jnp.float32)
    flat_memory = memory.reshape(total_rows, LONG, D).astype(jnp.float32)
    flat_cotangent = cotangent.reshape(total_rows, LONG, D).astype(jnp.float32)
    row_bucket = jnp.repeat(bucket, ROWS, axis=1).reshape(total_rows)
    flat_target = target_count.reshape(total_rows, QUARTERS)
    flat_counts = memory_count.reshape(total_rows, QUARTERS)

    def step_rows(totals, inputs):
        token_rows, memory_rows, cotangent_rows, bucket_value, target_counts, memory_counts = inputs
        self_mask, cross_mask = row_masks(bucket_value, target_counts, memory_counts)

        def forward(param_tuple, hidden, memory_part):
            return layer_row(param_tuple, hidden, memory_part, self_mask, cross_mask)
        result, backward = jax.vjp(forward, params, token_rows, memory_rows)
        param_grads, token_grads, memory_grads = backward(cotangent_rows)
        totals = jax.tree.map(jnp.add, totals, param_grads)
        return (totals, (result.astype(jnp.bfloat16), token_grads, memory_grads))
    starting = tuple((jnp.zeros_like(entry) for entry in params))
    totals, (outputs, token_grads, memory_grads) = lax.scan(step_rows, starting, (flat_tokens, flat_memory, flat_cotangent, row_bucket, flat_target, flat_counts))
    shape_all = (MICRO, NROWS, LONG, D)
    return (outputs.reshape(shape_all), token_grads.reshape(shape_all), memory_grads.reshape(shape_all), totals[0], totals[1], totals[2], totals[3], totals[4], totals[5], totals[6], totals[7], totals[8], totals[9], totals[10], totals[11], totals[12], totals[13], totals[14], totals[15], totals[16], totals[17], totals[18], totals[19], totals[20])
```

```python
import jax
import jax.numpy as jnp
from jax import lax
from jax.experimental import pallas as pl
from jax.experimental.pallas import tpu as pltpu
from jax.sharding import PartitionSpec as P

HD = 64
PAIR = 2 * HD
NEG = -1e30
BIG = 1e30
BH = ("batch", "head")
F32 = jnp.float32
BF16 = jnp.bfloat16


def plain_dot(left, right):
    return jnp.dot(left, right, preferred_element_type=F32)


def lower_dot(left, right):
    return lax.dot_general(left, right, (((0,), (0,)), ((), ())), preferred_element_type=F32)


def back_dot(left, right):
    return lax.dot_general(left, right, (((1,), (1,)), ((), ())), preferred_element_type=F32)


def pair_masks(value):
    lane = lax.broadcasted_iota(jnp.int32, value.shape, 1)
    zero = jnp.zeros_like(value)
    return (jnp.where(lane < HD, value, zero), jnp.where(lane >= HD, value, zero))


def block_mask(causal, block, shape, count):
    key_slot = lax.broadcasted_iota(jnp.int32, shape, 0)
    live = key_slot < count
    if causal:
        return live & (key_slot <= lax.broadcasted_iota(jnp.int32, shape, 1))
    return live


def visibility(causal, block, quarter, short):
    if block == 0:
        return None
    if causal:
        return jnp.logical_and(jnp.logical_not(short), (quarter ^ block) < quarter)
    return jnp.logical_not(short)


def forward_kernel(causal, blocks, meta, bucket, counts, q_ref, k_ref, v_ref, o_ref, lse_ref):
    unit = pl.program_id(0)
    quarter = meta[0]
    short = bucket[unit] == 1
    quarters = k_ref.shape[0]
    slots = q_ref.shape[1]

    def run(block_list):
        heads = pair_masks(q_ref[0])
        turned = [jnp.transpose(v_ref[j, 0]) for j in block_list]
        out = []
        for head, query in enumerate(heads):
            scores = []
            highest = None
            shown = []
            for j in block_list:
                score = back_dot(k_ref[j, 0], query)
                if j == 0 or not causal:
                    count = counts[unit * quarters + (quarter ^ j)]
                    score = jnp.where(block_mask(causal, j, score.shape, count), score, NEG)
                top = jnp.max(score, axis=0, keepdims=True)
                seen = visibility(causal, j, quarter, short)
                if seen is not None:
                    top = jnp.where(seen, top, NEG)
                shown.append(seen)
                highest = top if highest is None else jnp.maximum(highest, top)
                scores.append(score)
            total = jnp.zeros_like(highest)
            mixed = jnp.zeros((HD, slots), F32)
            for at, j in enumerate(block_list):
                limit = highest if shown[at] is None else jnp.where(shown[at], highest, BIG)
                raised = jnp.exp(scores[at] - limit)
                total = total + jnp.sum(raised, axis=0, keepdims=True)
                mixed = mixed + plain_dot(
                    turned[at][head * HD : (head + 1) * HD], raised.astype(BF16)
                )
            out.append(mixed * (1.0 / total))
            lse_ref[0, 0, head : head + 1, :] = highest + jnp.log(total)
        o_ref[0] = jnp.transpose(jnp.concatenate(out, axis=0)).astype(BF16)

    @pl.when(short)
    def _():
        run([0])

    @pl.when(jnp.logical_not(short))
    def _():
        run(list(range(quarters)))


def backward_kernel(
    causal, blocks, meta, bucket, counts, q_ref, k_ref, v_ref, o_ref, g_ref, lse_ref,
    dq_ref, dk_ref, dv_ref,
):
    unit = pl.program_id(0)
    quarter = meta[0]
    short = bucket[unit] == 1
    quarters = k_ref.shape[0]
    slots = q_ref.shape[1]

    def run(block_list):
        queries = pair_masks(q_ref[0])
        grads = pair_masks(g_ref[0])
        product = jnp.transpose(g_ref[0].astype(F32) * o_ref[0].astype(F32))
        turned = [jnp.transpose(k_ref[j, 0]) for j in block_list]
        query_grad = []
        key_grad = [None] * len(block_list)
        value_grad = [None] * len(block_list)
        for head in range(2):
            inner = jnp.sum(product[head * HD : (head + 1) * HD], axis=0, keepdims=True)
            total = lse_ref[0, 0, head : head + 1, :]
            query_part = jnp.zeros((HD, slots), F32)
            for at, j in enumerate(block_list):
                score = back_dot(k_ref[j, 0], queries[head])
                if j == 0 or not causal:
                    count = counts[unit * quarters + (quarter ^ j)]
                    score = jnp.where(block_mask(causal, j, score.shape, count), score, NEG)
                seen = visibility(causal, j, quarter, short)
                limit = total if seen is None else jnp.where(seen, total, BIG)
                probs = jnp.exp(score - limit)
                probs_grad = back_dot(v_ref[j, 0], grads[head])
                score_grad = (probs * (probs_grad - inner)).astype(BF16)
                key_part = plain_dot(score_grad, queries[head])
                value_part = plain_dot(probs.astype(BF16), grads[head])
                query_part = query_part + plain_dot(
                    turned[at][head * HD : (head + 1) * HD], score_grad
                )
                if head == 0:
                    key_grad[at] = key_part
                    value_grad[at] = value_part
                else:
                    dk_ref[j, 0] = (key_grad[at] + key_part).astype(BF16)
                    dv_ref[j, 0] = (value_grad[at] + value_part).astype(BF16)
            query_grad.append(query_part)
        dq_ref[0] = (jnp.transpose(jnp.concatenate(query_grad, axis=0)) * 0.125).astype(BF16)

    @pl.when(short)
    def _():
        run([0])
        for j in range(1, quarters):
            dk_ref[j, 0] = jnp.zeros(dk_ref.shape[2:], BF16)
            dv_ref[j, 0] = jnp.zeros(dv_ref.shape[2:], BF16)

    @pl.when(jnp.logical_not(short))
    def _():
        run(list(range(quarters)))


def attention_specs(units, quarters, slots, width):
    pairs = width // PAIR
    query = pl.BlockSpec((1, slots, PAIR), lambda u, p, *_: (u, 0, p))
    key = pl.BlockSpec((quarters, 1, slots, PAIR), lambda u, p, *_: (0, u, 0, p))
    value = pl.BlockSpec((quarters, 1, slots, PAIR), lambda u, p, *_: (0, u, 0, pairs + p))
    lse = pl.BlockSpec((1, 1, 8, slots), lambda u, p, *_: (u, p, 0, 0))
    return pairs, query, key, value, lse


def attention_cost(units, quarters, slots, width, matmuls):
    cells = units * quarters * slots * slots * (width // HD)
    return pl.CostEstimate(
        flops=2 * cells * HD * matmuls,
        transcendentals=cells,
        bytes_accessed=units * slots * width * 2 * (2 + 2 * quarters),
    )


def attend_forward(causal, meta, bucket, counts, query, keys):
    units, slots, width = query.shape
    quarters = keys.shape[0]
    pairs, q_spec, k_spec, v_spec, lse_spec = attention_specs(units, quarters, slots, width)

    def kernel(*refs):
        forward_kernel(causal, quarters, *refs)

    return pl.pallas_call(
        kernel,
        grid_spec=pltpu.PrefetchScalarGridSpec(
            num_scalar_prefetch=3,
            grid=(units, pairs),
            in_specs=[q_spec, k_spec, v_spec],
            out_specs=[q_spec, lse_spec],
        ),
        out_shape=[
            jax.ShapeDtypeStruct((units, slots, width), BF16),
            jax.ShapeDtypeStruct((units, pairs, 8, slots), F32),
        ],
        cost_estimate=attention_cost(units, quarters, slots, width, 2),
        name="self_forward" if causal else "cross_forward",
    )(meta, bucket, counts, query, keys, keys)


def attend_backward(causal, meta, bucket, counts, query, keys, mixed, grad, lse):
    units, slots, width = query.shape
    quarters = keys.shape[0]
    pairs, q_spec, k_spec, v_spec, lse_spec = attention_specs(units, quarters, slots, width)

    def kernel(*refs):
        backward_kernel(causal, quarters, *refs)

    return pl.pallas_call(
        kernel,
        grid_spec=pltpu.PrefetchScalarGridSpec(
            num_scalar_prefetch=3,
            grid=(units, pairs),
            in_specs=[q_spec, k_spec, v_spec, q_spec, q_spec, lse_spec],
            out_specs=[q_spec, k_spec, k_spec],
        ),
        out_shape=[
            jax.ShapeDtypeStruct((units, slots, width), BF16),
            jax.ShapeDtypeStruct((quarters, units, slots, width), BF16),
            jax.ShapeDtypeStruct((quarters, units, slots, width), BF16),
        ],
        cost_estimate=attention_cost(units, quarters, slots, width, 5),
        name="self_backward" if causal else "cross_backward",
    )(meta, bucket, counts, query, keys, keys, mixed, grad, lse)


def norm_forward(value, gain, shift):
    centre = value - jnp.mean(value, axis=-1, keepdims=True)
    spread = jnp.mean(centre * centre, axis=-1, keepdims=True)
    scale = lax.rsqrt(spread + 1e-05)
    unit = centre * scale
    return unit * gain + shift, unit, scale


def norm_backward(grad, unit, scale, gain):
    scaled = grad * gain
    mean = jnp.mean(scaled, axis=-1, keepdims=True)
    along = jnp.mean(scaled * unit, axis=-1, keepdims=True)
    back = scale * (scaled - mean - unit * along)
    return back, jnp.sum(grad * unit, axis=0), jnp.sum(grad, axis=0)


def column_blocks(shard, width):
    rows = shard.shape[0]
    return [shard[:, at : at + width] for at in range(0, shard.shape[1], width)]


def row_blocks(shard, rows):
    return [shard[at : at + rows] for at in range(0, shard.shape[0], rows)]


def body(
    tokens, memory, cotangent, bucket, target_count, memory_count,
    self_weight, query_bias, value_bias, attend_weight, attend_bias, first_gain, first_shift,
    cross_query, cross_bias, memory_weight, memory_bias, cross_weight, crossed_bias,
    second_gain, second_shift, expand_weight, expand_bias, reduce_weight, reduce_bias,
    third_gain, third_shift,
):
    micro_count, row_count, slots, width = tokens.shape
    units = micro_count * row_count
    heads = lax.axis_size("head")
    devices = lax.axis_size("batch") * heads
    quarter = lax.axis_index("head").astype(jnp.int32)
    inner_width = expand_weight.shape[1]
    folds = inner_width // width
    shard_rows = attend_weight.shape[0]
    own = units * slots

    meta = quarter.reshape(1)
    bucket_units = jnp.repeat(bucket.reshape(micro_count), row_count)
    target_units = target_count.reshape(-1)
    memory_units = memory_count.reshape(-1)

    def swap(value, step):
        return lax.ppermute(value, "head", [(i, i ^ step) for i in range(heads)])

    def gather_quarters(value):
        parts = [value]
        step = heads // 2
        others = {0: value}
        while step >= 1:
            for known in list(others):
                others[known | step] = swap(others[known], step)
            step //= 2
        return jnp.stack([others[j] for j in range(heads)])

    own_tokens = tokens.reshape(units, slots, width)
    own_memory = memory.reshape(units, slots, width)
    all_tokens = gather_quarters(own_tokens)
    all_memory = gather_quarters(own_memory)

    bias_names = [
        query_bias, value_bias, attend_bias, first_gain, first_shift, cross_bias, memory_bias,
        crossed_bias, second_gain, second_shift, reduce_bias, third_gain, third_shift,
    ]
    flat_bias = jnp.concatenate(bias_names + [expand_bias])
    bias_size = flat_bias.shape[0]
    bias_rows = -(-bias_size // width)
    padded = jnp.pad(flat_bias, (0, bias_rows * width - bias_size)).reshape(bias_rows, width)
    near_blocks = (
        column_blocks(self_weight, width)
        + column_blocks(memory_weight, width)
        + [attend_weight, cross_query, cross_weight]
    )
    near = jnp.concatenate(near_blocks + [padded], axis=0)
    far = jnp.concatenate(
        column_blocks(expand_weight, width) + row_blocks(reduce_weight, shard_rows), axis=0
    )
    near_all = lax.all_gather(near, BH, axis=0, tiled=False)
    far_all = lax.all_gather(far, BH, axis=0, tiled=False)

    def near_chunk(at, count=1):
        return near_all[:, at * shard_rows : (at + count) * shard_rows, :].reshape(
            devices * shard_rows * count, width
        )

    w_q, w_k, w_v, w_mk, w_mv, w_att, w_cq, w_cw = [near_chunk(at) for at in range(8)]
    w_kv = jnp.concatenate([w_k, w_v], axis=1)
    w_mkv = jnp.concatenate([w_mk, w_mv], axis=1)
    bias_all = near_all[:, 8 * shard_rows :, :].reshape(devices, bias_rows * width)
    bias_vec = [
        bias_all[:, at * shard_rows : (at + 1) * shard_rows].reshape(1, width).astype(F32)
        for at in range(13)
    ]
    (
        b_q, b_v, b_att, g_1, s_1, b_cq, b_mv, b_cw, g_2, s_2, b_red, g_3, s_3,
    ) = bias_vec
    b_exp = (
        bias_all[:, 13 * shard_rows : bias_size].reshape(1, inner_width).astype(F32)
    )
    w_exp = jnp.concatenate(
        [
            far_all[:, at * shard_rows : (at + 1) * shard_rows, :].reshape(width, width)
            for at in range(folds)
        ],
        axis=1,
    )
    w_red = far_all[:, folds * shard_rows :, :].reshape(inner_width, width)

    x = own_tokens.reshape(own, width)
    flat_all = all_tokens.reshape(heads * own, width)
    flat_memory = all_memory.reshape(heads * own, width)
    zero = jnp.zeros((1, width), F32)
    query = ((plain_dot(x, w_q) + b_q).astype(BF16) * 0.125).astype(BF16)
    keys = (plain_dot(flat_all, w_kv) + jnp.concatenate([zero, b_v], axis=1)).astype(BF16)
    memory_keys = (plain_dot(flat_memory, w_mkv) + jnp.concatenate([zero, b_mv], axis=1)).astype(
        BF16
    )
    query = query.reshape(units, slots, width)
    keys = keys.reshape(heads, units, slots, 2 * width)
    memory_keys = memory_keys.reshape(heads, units, slots, 2 * width)
    mixed, self_lse = attend_forward(True, meta, bucket_units, target_units, query, keys)
    flat_mixed = mixed.reshape(own, width)
    first_sum = x.astype(F32) + plain_dot(flat_mixed, w_att) + b_att
    first, unit_1, scale_1 = norm_forward(first_sum, g_1, s_1)
    first_low = first.astype(BF16)
    cross_q = ((plain_dot(first_low, w_cq) + b_cq).astype(BF16) * 0.125).astype(BF16)
    cross_q = cross_q.reshape(units, slots, width)
    crossed, cross_lse = attend_forward(
        False, meta, bucket_units, memory_units, cross_q, memory_keys
    )
    flat_crossed = crossed.reshape(own, width)
    second_sum = first + plain_dot(flat_crossed, w_cw) + b_cw
    second, unit_2, scale_2 = norm_forward(second_sum, g_2, s_2)
    second_low = second.astype(BF16)
    inner = plain_dot(second_low, w_exp) + b_exp
    share = 0.5 * (1.0 + lax.erf(inner * 0.7071067811865476))
    density = jnp.exp(-0.5 * inner * inner) * 0.3989422804014327
    active = (inner * share).astype(BF16)
    slope = (share + inner * density).astype(BF16)
    third_sum = second + plain_dot(active, w_red) + b_red
    result, unit_3, scale_3 = norm_forward(third_sum, g_3, s_3)
    output = result.astype(BF16).reshape(tokens.shape)

    upstream = cotangent.reshape(own, width).astype(F32)
    third_grad, dg_3, ds_3 = norm_backward(upstream, unit_3, scale_3, g_3)
    feed_low = third_grad.astype(BF16)
    d_red = lower_dot(active, feed_low).astype(BF16)
    db_red = jnp.sum(feed_low.astype(F32), axis=0)
    inner_low = (back_dot(feed_low, w_red) * slope.astype(F32)).astype(BF16)
    d_exp = lower_dot(second_low, inner_low).astype(BF16)
    db_exp = jnp.sum(inner_low.astype(F32), axis=0)
    second_total = third_grad + back_dot(inner_low, w_exp)
    second_grad, dg_2, ds_2 = norm_backward(second_total, unit_2, scale_2, g_2)
    cross_low = second_grad.astype(BF16)
    d_cw = lower_dot(flat_crossed, cross_low).astype(BF16)
    db_cw = jnp.sum(cross_low.astype(F32), axis=0)
    crossed_grad = back_dot(cross_low, w_cw).astype(BF16).reshape(units, slots, width)
    d_cross_q, d_mk, d_mv = attend_backward(
        False, meta, bucket_units, memory_units, cross_q, memory_keys, crossed, crossed_grad,
        cross_lse,
    )
    flat_dcq = d_cross_q.reshape(own, width)
    d_cq = lower_dot(first_low, flat_dcq).astype(BF16)
    db_cq = jnp.sum(flat_dcq.astype(F32), axis=0)
    first_total = second_grad + back_dot(flat_dcq, w_cq)
    first_grad, dg_1, ds_1 = norm_backward(first_total, unit_1, scale_1, g_1)
    attend_low = first_grad.astype(BF16)
    d_att = lower_dot(flat_mixed, attend_low).astype(BF16)
    db_att = jnp.sum(attend_low.astype(F32), axis=0)
    mixed_grad = back_dot(attend_low, w_att).astype(BF16).reshape(units, slots, width)
    flat_dmk = d_mk.reshape(heads * own, width)
    flat_dmv = d_mv.reshape(heads * own, width)
    d_mkw = lower_dot(flat_memory, flat_dmk).astype(BF16)
    d_mvw = lower_dot(flat_memory, flat_dmv).astype(BF16)
    db_mv = jnp.sum(flat_dmv.astype(F32), axis=0)
    memory_part = (back_dot(flat_dmk, w_mk) + back_dot(flat_dmv, w_mv)).reshape(
        heads, units, slots, width
    )
    d_q, d_k, d_v = attend_backward(
        True, meta, bucket_units, target_units, query, keys, mixed, mixed_grad, self_lse
    )
    flat_dq = d_q.reshape(own, width)
    flat_dk = d_k.reshape(heads * own, width)
    flat_dv = d_v.reshape(heads * own, width)
    d_qw = lower_dot(x, flat_dq).astype(BF16)
    d_kw = lower_dot(flat_all, flat_dk).astype(BF16)
    d_vw = lower_dot(flat_all, flat_dv).astype(BF16)
    db_q = jnp.sum(flat_dq.astype(F32), axis=0)
    db_v = jnp.sum(flat_dv.astype(F32), axis=0)
    token_part = (back_dot(flat_dk, w_k) + back_dot(flat_dv, w_v)).reshape(
        heads, units, slots, width
    )
    token_own = (first_grad + back_dot(flat_dq, w_q)).reshape(units, slots, width)

    def scatter_quarters(parts, extra):
        held = {j: parts[j].astype(BF16) for j in range(1, heads)}
        held[0] = parts[0] if extra is None else parts[0] + extra
        step = 1
        while step < heads:
            kept = {}
            for j in held:
                if not j & step:
                    moved = swap(held[j | step], step).astype(F32)
                    total = held[j].astype(F32) + moved
                    kept[j] = total if j == 0 else total.astype(BF16)
            held = kept
            step *= 2
        return held[0]

    memory_grad = scatter_quarters(memory_part, None).reshape(memory.shape)
    tokens_grad = scatter_quarters(token_part, token_own).reshape(tokens.shape)

    def shards(full):
        return full.reshape(devices, shard_rows, width)

    far_grad = jnp.concatenate(
        [shards(d_exp[:, at * width : (at + 1) * width]) for at in range(folds)]
        + [d_red.reshape(devices, folds * shard_rows, width)],
        axis=1,
    )
    bias_grads = [
        db_q, db_v, db_att, dg_1, ds_1, db_cq, db_mv, db_cw, dg_2, ds_2, db_red, dg_3, ds_3,
    ]
    bias_grad = jnp.concatenate(
        [one.reshape(devices, shard_rows) for one in bias_grads]
        + [db_exp.reshape(devices, inner_width // devices)],
        axis=1,
    ).astype(BF16)
    bias_grad = jnp.pad(bias_grad, ((0, 0), (0, bias_rows * width - bias_size))).reshape(
        devices, bias_rows, width
    )
    near_grad = jnp.concatenate(
        [shards(one) for one in (d_qw, d_kw, d_vw, d_mkw, d_mvw, d_att, d_cq, d_cw)]
        + [bias_grad],
        axis=1,
    )
    far_sum = lax.psum_scatter(far_grad, BH, scatter_dimension=0, tiled=False).astype(F32)
    near_sum = lax.psum_scatter(near_grad, BH, scatter_dimension=0, tiled=False).astype(F32)

    def near_rows(at):
        return near_sum[at * shard_rows : (at + 1) * shard_rows]

    bias_sum = near_sum[8 * shard_rows :].reshape(bias_rows * width)

    def bias_out(at):
        return bias_sum[at * shard_rows : (at + 1) * shard_rows]

    self_out = jnp.concatenate([near_rows(0), near_rows(1), near_rows(2)], axis=1)
    memory_out = jnp.concatenate([near_rows(3), near_rows(4)], axis=1)
    expand_out = jnp.concatenate(
        [far_sum[at * shard_rows : (at + 1) * shard_rows] for at in range(folds)], axis=1
    )
    reduce_out = far_sum[folds * shard_rows :]
    return (
        output, tokens_grad, memory_grad,
        self_out, bias_out(0), bias_out(1), near_rows(5), bias_out(2), bias_out(3), bias_out(4),
        near_rows(6), bias_out(5), memory_out, bias_out(6), near_rows(7), bias_out(7),
        bias_out(8), bias_out(9), expand_out, bias_sum[13 * shard_rows : bias_size],
        reduce_out, bias_out(10), bias_out(11), bias_out(12),
    )


def solution(mesh):
    rows = P(None, "batch", "head", None)
    matrix = P(BH, None)
    vector = P(BH)
    weights = (
        matrix, vector, vector, matrix, vector, vector, vector, matrix, vector, matrix, vector,
        matrix, vector, vector, vector, matrix, vector, matrix, vector, vector, vector,
    )
    return jax.shard_map(
        body,
        mesh=mesh,
        in_specs=(rows, rows, rows, P(None, "batch"), P(None, "batch", None), P(None, "batch", None))
        + weights,
        out_specs=(rows, rows, rows) + weights,
        check_vma=False,
    )
```
